32 devices in a mesh: grp: 2 (over x), seq: 8 (over z, y), rep: 2 (over core).
Axes of the slice: x: 2, y: 2, z: 4, core: 2. Of those that a mesh axis runs over, the one named last changes fastest.
Arguments:
- queries: bfloat16 [4, 2048, 1024], P(('grp', 'rep'), None, 'seq'), parts along dimension 0, may hold values from -60 to 60
- key_vectors: bfloat16 [4, 2048, 1024], P(('grp', 'rep'), None, 'seq'), parts along dimension 0, may hold values from -8 to 8
- value_vectors: bfloat16 [4, 2048, 1024], P(('grp', 'rep'), None, 'seq'), parts along dimension 0, may hold values from -6 to 6
- context: bfloat16 [4, 2048, 1024], P(('grp', 'rep'), None, 'seq'), parts along dimension 0, may hold values from -6 to 6
- cotangent: bfloat16 [4, 2048, 1024], P(('grp', 'rep'), None, 'seq'), parts along dimension 0, may hold values from -6 to 6
- out_weight: bfloat16 [4096, 2048], P('grp'), parts along dimension 0, may hold values from -0.125 to 0.125
- membership: int32 [4, 1024], P(('grp', 'rep'), 'seq'), parts along dimension 0, may hold values from 0 to 1, as said below
Outputs:
- grad_queries: bfloat16 [4, 2048, 1024], P(('grp', 'rep'), None, 'seq'), parts along dimension 0
- grad_keys: bfloat16 [4, 2048, 1024], P(('grp', 'rep'), None, 'seq'), parts along dimension 0
- grad_values: bfloat16 [4, 2048, 1024], P(('grp', 'rep'), None, 'seq'), parts along dimension 0
- grad_weight: float32 [4096, 2048], P(('grp', 'seq', 'rep')), parts along dimension 0
The draws below stay inside these ranges and needn't reach their ends.
There are 2 independent parts, one for each index of `grp`. The reference program is written for one: setup_inputs(seed, part) draws one part's arguments, and reference() takes and returns one part's arrays. A program takes and returns all parts, laid end to end along the dimension named above; each array names one. Nothing has to cross between parts.
Inputs may be any that keep to these rules, and one draw needn't show every extreme that they name: Every window has at least one cell with membership 1.
All inputs are finite; a program needn't handle non-finite values.
Results may differ from the reference program's by a relative error of at most 0.0058.
Values may be sent and summed in bfloat16 or wider, within the bound.
A program may use at most 128 MiB of HBM per device.

```python
import math
import jax
import jax.numpy as jnp
from jax import lax

HEADS = 32
DH = 64
D = 2048
WINDOW_CELLS = 1024
WINDOW_REPLICAS = 2


def draw_pair(key):
    random_root_key = jax.random.fold_in(key, 91)
    random_query_draw, random_key_draw, random_query_scale, random_key_scale = jax.random.split(random_root_key, 4)
    shape = (WINDOW_REPLICAS, D, WINDOW_CELLS)
    query_base = jax.random.truncated_normal(random_query_draw, -4.0, 4.0, shape, jnp.float32)
    key_base = jax.random.truncated_normal(random_key_draw, -4.0, 4.0, shape, jnp.float32)
    query_scale = jnp.exp(jax.random.uniform(random_query_scale, (WINDOW_REPLICAS, 1, WINDOW_CELLS), jnp.float32, math.log(0.5), math.log(2.0)))
    random_scale_draw = jnp.exp(jax.random.uniform(random_key_scale, (WINDOW_REPLICAS, 1, WINDOW_CELLS), jnp.float32, math.log(0.5), math.log(2.0)))
    key_out = key_base * random_scale_draw
    query_out = query_base * query_scale
    return (query_out, key_out)


def draw_queries(key, part):
    return draw_pair(key)[0].astype(jnp.bfloat16)


def draw_key_vectors(key, part):
    return draw_pair(key)[1].astype(jnp.bfloat16)


def draw_membership(key, part):
    random_root_key = jax.random.fold_in(key, 53)
    key_coin, key_chosen = jax.random.split(random_root_key, 2)
    coin_flip = jax.random.randint(key_coin, (WINDOW_REPLICAS, WINDOW_CELLS), 0, 8)
    chosen = jax.random.randint(key_chosen, (WINDOW_REPLICAS, 1), 0, WINDOW_CELLS)
    cell_ids = jnp.arange(WINDOW_CELLS, dtype=jnp.int32)
    return jnp.where((coin_flip > 0) | (cell_ids[None, :] == chosen), 1, 0).astype(jnp.int32)


def raised(drawn, own_key, source, target, blocks, factor):
    def block_of(position):
        return (jnp.arange(drawn.shape[position]) // (drawn.shape[position] // blocks)).reshape((-1,) + (1,) * (drawn.ndim - 1 - position))

    first = jax.random.permutation(own_key, blocks)[block_of(target)]
    second = (block_of(target) + blocks // 2) % blocks
    return jnp.where((block_of(source) == first) | (block_of(source) == second), factor * drawn, drawn)


def steps_of(key, extent, pieces, smallest, high):
    def one(dim, shards_of):
        draws = jax.random.uniform(jax.random.fold_in(jax.random.fold_in(key, 6), dim), (shards_of,), jnp.float32, smallest / len(pieces), high / len(pieces))
        return jnp.repeat(jnp.exp(draws), extent[dim] // shards_of).reshape((-1,) + (1,) * (len(extent) - dim - 1))

    factor_of = one(*pieces[0])
    for cut in pieces[1:]:
        factor_of = factor_of * one(*cut)
    return factor_of


def centred(own_key, extent, spread, reach, pieces=(), kind=jnp.bfloat16):
    drawn = jax.random.normal(own_key, extent, jnp.float32) * spread
    if len(pieces) > 0:
        drawn = steps_of(own_key, extent, pieces, -0.22, 0.18) * drawn
    return jnp.clip(drawn, min=-reach, max=reach).astype(kind)


def gaussian_with(own_key, shape, deviation, reach, cuts, heavy, kind=jnp.bfloat16):
    values = deviation * jax.random.normal(own_key, shape, jnp.float32)
    if cuts:
        values = values * steps_of(own_key, shape, cuts, -0.22, 0.18)
    return jnp.clip(raised(values, jax.random.fold_in(own_key, 3), *heavy), -reach, reach).astype(kind)


def setup_inputs(seed: int = 0, part: int = 0) -> dict:
    keys = jax.random.split(jax.random.key(seed), 8)
    own_keys = jax.random.split(jax.random.fold_in(keys[7], part), 8)
    queries = draw_queries(jax.random.fold_in(jax.random.fold_in(keys[7], part), 71), part)
    key_vectors = draw_key_vectors(jax.random.fold_in(jax.random.fold_in(keys[7], part), 71), part)
    value_vectors = centred(own_keys[2], (WINDOW_REPLICAS, D, WINDOW_CELLS), 1.0, 6.0, ((0, 2), (2, 8)))
    context = gaussian_with(own_keys[3], (WINDOW_REPLICAS, D, WINDOW_CELLS), 1.0, 6.0, ((0, 2), (2, 8)), (2, 1, 8, 2.0))
    cotangent = centred(own_keys[4], (WINDOW_REPLICAS, D, WINDOW_CELLS), 1.0, 6.0, ((0, 2), (2, 8)))
    out_weight = centred(own_keys[5], (D, D), D ** -0.5, 0.125)
    membership = draw_membership(jax.random.fold_in(jax.random.fold_in(keys[7], part), 71), part)
    return {"queries": queries, "key_vectors": key_vectors, "value_vectors": value_vectors, "context": context, "cotangent": cotangent, "out_weight": out_weight, "membership": membership}


def head_grads(query_head, key_head, value_head, grad_head, context_head, member_keys):
    score_scale = 1.0 / math.sqrt(DH)
    scores = jnp.dot(query_head.T, key_head, preferred_element_type=jnp.float32) * score_scale
    scores = jnp.where(member_keys[None, :], scores, -jnp.inf)
    highest = lax.optimization_barrier(jnp.max(scores, axis=1, keepdims=True))
    exp_scores = jnp.exp(scores - highest)
    probabilities = exp_scores / lax.optimization_barrier(jnp.sum(exp_scores, axis=1, keepdims=True))
    row_delta = lax.optimization_barrier(jnp.sum(grad_head.astype(jnp.float32) * context_head.astype(jnp.float32), axis=0))
    probs_low = probabilities.astype(jnp.bfloat16)
    grad_value = jnp.dot(grad_head, probs_low, preferred_element_type=jnp.float32).astype(jnp.bfloat16)
    grad_probs = jnp.dot(grad_head.T, value_head, preferred_element_type=jnp.float32)
    grad_scores = (probabilities * (grad_probs - row_delta[:, None]) * score_scale).astype(jnp.bfloat16)
    grad_query = jnp.dot(key_head, grad_scores.T, preferred_element_type=jnp.float32).astype(jnp.bfloat16)
    grad_key = jnp.dot(query_head, grad_scores, preferred_element_type=jnp.float32).astype(jnp.bfloat16)
    return (grad_query, grad_key, grad_value)

def reference(queries, key_vectors, value_vectors, context, cotangent, out_weight, membership):
    grad_context = jnp.stack([jnp.dot(out_weight, cotangent[replica], preferred_element_type=jnp.float32).astype(jnp.bfloat16) for replica in range(WINDOW_REPLICAS)])
    zero_index = jnp.zeros((), jnp.int32)

    def one_pair(pair_index):
        replica = (pair_index // HEADS).astype(jnp.int32)
        head_index = (pair_index % HEADS).astype(jnp.int32)
        first_row = (head_index * DH).astype(jnp.int32)

        def select(array):
            return lax.dynamic_slice(array, (replica, first_row, zero_index), (1, DH, WINDOW_CELLS))[0]
        member_keys = lax.dynamic_index_in_dim(membership, replica, 0, keepdims=False) > 0
        return head_grads(select(queries), select(key_vectors), select(value_vectors), select(grad_context), select(context), member_keys)
    results = lax.map(one_pair, jnp.arange(WINDOW_REPLICAS * HEADS, dtype=jnp.int32))
    grad_queries = results[0].reshape(WINDOW_REPLICAS, D, WINDOW_CELLS)
    grad_keys = results[1].reshape(WINDOW_REPLICAS, D, WINDOW_CELLS)
    grad_values = results[2].reshape(WINDOW_REPLICAS, D, WINDOW_CELLS)
    grad_weight = jnp.zeros((D, D), jnp.float32)
    for replica in range(WINDOW_REPLICAS):
        grad_weight = grad_weight + jnp.dot(context[replica], cotangent[replica].T, preferred_element_type=jnp.float32)
    return (grad_queries, grad_keys, grad_values, grad_weight)
```

```python
import functools
import math

import jax
import jax.numpy as jnp
from jax import lax
from jax.experimental import pallas as pl
from jax.experimental.pallas import tpu as pltpu
from jax.sharding import PartitionSpec as P

DH = 64
MESH = pl.DeviceIdType.MESH
CHUNKS = 2


def kernel(n, ny, *refs):
    (q_ref, k_ref, v_ref, c_ref, cot_ref, w_ref, m_ref,
     dq_out, dk_out, dv_out, gw_out,
     q_buf, k_buf, v_buf, c_buf, g_buf, dq_buf, dk_buf, dv_buf,
     cot, w_buf, m_buf, gw, gw_in, k_acc, v_acc,
     w_sem, own_sem, m_send, m_recv, in_send, in_recv,
     ag_send, ag_recv, out_send, out_recv, gw_send, gw_recv) = refs
    me = lax.axis_index("seq")
    rep = lax.axis_index("rep")
    nz = n // ny
    z, y = me // ny, me % ny
    rows, length = q_buf.shape
    cells = length // n
    features = cot.shape[0]
    heads = rows // DH
    half = rows // 2
    piece = features // CHUNKS
    inputs = ((k_ref, k_buf), (q_ref, q_buf), (v_ref, v_buf), (c_ref, c_buf))
    outputs = ((dv_buf, dv_out), (dq_buf, dq_out), (dk_buf, dk_out))

    def cols(seq):
        return pl.ds(pl.multiple_of(seq * cells, cells), cells)

    def head_rows(h, owner=0):
        return pl.ds(pl.multiple_of(owner * rows + h * DH, DH), DH)

    barrier = pltpu.get_barrier_semaphore()
    for k in range(1, n):
        pl.semaphore_signal(barrier, inc=1, device_id={"seq": (me + k) % n}, device_id_type=MESH)
    pl.semaphore_signal(barrier, inc=1, device_id={"rep": 1 - rep}, device_id_type=MESH)

    w_copy = pltpu.make_async_copy(
        w_ref.at[pl.ds(pl.multiple_of(me * rows, rows), rows), :], w_buf, w_sem
    )
    w_copy.start()
    own_copy = pltpu.make_async_copy(cot_ref.at[0], cot.at[:, cols(me)], own_sem)
    own_copy.start()
    pltpu.make_async_copy(m_ref, m_buf.at[:, cols(me)], m_recv).start()

    pl.semaphore_wait(barrier, n)

    def ag_copy(step, part, origin, way, target):
        part_rows = pl.ds(part * piece, piece)
        landing = cot.at[part_rows, cols(origin)]
        source = cot_ref.at[0, part_rows, :] if step == 0 else landing
        return pltpu.make_async_remote_copy(
            src_ref=source,
            dst_ref=landing,
            send_sem=ag_send.at[way, step, part],
            recv_sem=ag_recv.at[part, origin],
            device_id={"seq": target},
            device_id_type=MESH,
        )

    def ag_wait(part, origin):
        landing = cot.at[pl.ds(part * piece, piece), cols(origin)]
        pltpu.make_async_copy(landing, landing, ag_recv.at[part, origin]).wait()

    def ag_step(step, arrived, send):
        for part in range(CHUNKS):
            up, down = z - step, z + step

            def act(origin, way, target):
                copy = ag_copy(step, part, origin, way, target)
                if send:
                    copy.start()
                else:
                    copy.wait_send()

            def cross(origin, way):
                if ny == 2:
                    act(origin, way, z * ny + 1 - y)

            @pl.when(up >= 0)
            def _():
                if arrived:
                    ag_wait(part, up * ny + y)

                @pl.when(z + 1 < nz)
                def _():
                    act(up * ny + y, 0, me + ny)

                cross(up * ny + y, 2)

            @pl.when(down < nz)
            def _():
                if arrived:
                    ag_wait(part, down * ny + y)

                @pl.when(z >= 1)
                def _():
                    act(down * ny + y, 1, me - ny)

                if step > 0:
                    cross(down * ny + y, 3)

    def send_inputs(h):
        for t, (ref, buf) in enumerate(inputs):
            pltpu.make_async_copy(
                ref.at[0, head_rows(h, me), :], buf.at[head_rows(h), cols(me)], in_recv.at[t, h]
            ).start()

        def to_peer(k, carry):
            peer = (me + k) % n
            for t, (ref, buf) in enumerate(inputs):
                pltpu.make_async_remote_copy(
                    src_ref=ref.at[0, head_rows(h, peer), :],
                    dst_ref=buf.at[head_rows(h), cols(me)],
                    send_sem=in_send.at[t],
                    recv_sem=in_recv.at[t, h],
                    device_id={"seq": peer},
                    device_id_type=MESH,
                ).start()
            return carry

        lax.fori_loop(1, n, to_peer, 0)

    def send_members(k, carry):
        pltpu.make_async_remote_copy(
            src_ref=m_ref,
            dst_ref=m_buf.at[:, cols(me)],
            send_sem=m_send,
            recv_sem=m_recv,
            device_id={"seq": (me + k) % n},
            device_id_type=MESH,
        ).start()
        return carry

    sent = 0
    for step in range(nz):
        ag_step(step, arrived=step > 0, send=True)
        if step == 0:
            lax.fori_loop(1, n, send_members, 0)
        upto = -(-(step + 1) * heads // nz)
        for h in range(sent, upto):
            send_inputs(h)
        sent = upto
    if ny == 2:
        for origin_z in range(nz):
            for part in range(CHUNKS):
                ag_wait(part, origin_z * ny + 1 - y)
    own_copy.wait()
    w_copy.wait()

    block = min(256, length)

    def project(i, carry):
        at = pl.ds(pl.multiple_of(i * block, block), block)
        g_buf[:, at] = jnp.dot(
            w_buf[...], cot[:, at], preferred_element_type=jnp.float32
        ).astype(jnp.bfloat16)
        return carry

    lax.fori_loop(0, length // block, project, 0)
    pltpu.make_async_copy(m_buf, m_buf, m_recv).wait()

    scale = 1.0 / math.sqrt(DH)
    tile = 256 if length <= 2048 else 128

    def one_head(h, carry):
        mine = head_rows(h)
        for t, (_, buf) in enumerate(inputs):
            pltpu.make_async_copy(buf.at[mine], buf.at[mine], in_recv.at[t, h]).wait()
        member = m_buf[...] > 0
        keys = k_buf[mine, :]
        values = v_buf[mine, :]
        keys_scaled = keys * jnp.bfloat16(scale)
        k_acc[...] = jnp.zeros_like(k_acc)
        v_acc[...] = jnp.zeros_like(v_acc)

        def one_tile(i, inner):
            at = pl.ds(pl.multiple_of(i * tile, tile), tile)
            query = q_buf[mine, at] * jnp.bfloat16(scale)
            grad = g_buf[mine, at]
            products = grad.astype(jnp.float32) * c_buf[mine, at].astype(jnp.float32)
            delta = jnp.sum(products.T, axis=1, keepdims=True)
            first = (((0,), (0,)), ((), ()))
            scores = lax.dot_general(query, keys, first, preferred_element_type=jnp.float32)
            scores = jnp.where(member, scores, -jnp.inf)
            exps = jnp.exp(scores - jnp.max(scores, axis=1, keepdims=True))
            probs = exps * (1.0 / jnp.sum(exps, axis=1, keepdims=True))
            v_acc[...] += jnp.dot(
                grad, probs.astype(jnp.bfloat16), preferred_element_type=jnp.float32
            )
            grad_probs = lax.dot_general(grad, values, first, preferred_element_type=jnp.float32)
            grad_scores = (probs * (grad_probs - delta)).astype(jnp.bfloat16)
            dq_buf[mine, at] = lax.dot_general(
                keys_scaled, grad_scores, (((1,), (1,)), ((), ())),
                preferred_element_type=jnp.float32,
            ).astype(jnp.bfloat16)
            k_acc[...] += jnp.dot(query, grad_scores, preferred_element_type=jnp.float32)
            return inner

        lax.fori_loop(0, length // tile, one_tile, 0)
        dk_buf[mine, :] = k_acc[...].astype(jnp.bfloat16)
        dv_buf[mine, :] = v_acc[...].astype(jnp.bfloat16)
        for t, (buf, out) in enumerate(outputs):
            pltpu.make_async_copy(
                buf.at[mine, cols(me)], out.at[0, head_rows(h, me), :], out_recv.at[t]
            ).start()

        def to_peer(k, inner):
            peer = (me + k) % n
            for t, (buf, out) in enumerate(outputs):
                pltpu.make_async_remote_copy(
                    src_ref=buf.at[mine, cols(peer)],
                    dst_ref=out.at[0, head_rows(h, me), :],
                    send_sem=out_send.at[t],
                    recv_sem=out_recv.at[t],
                    device_id={"seq": peer},
                    device_id_type=MESH,
                ).start()
            return inner

        lax.fori_loop(1, n, to_peer, 0)
        return carry

    lax.fori_loop(0, heads, one_head, 0)

    width = min(256, features)

    def weight_part(i, carry):
        at = pl.ds(pl.multiple_of(i * width, width), width)
        gw[:, at] = lax.dot_general(
            c_buf[...], cot[at, :], (((1,), (1,)), ((), ())), preferred_element_type=jnp.float32
        )
        return carry

    lax.fori_loop(0, features // width, weight_part, 0)
    swap = pltpu.make_async_remote_copy(
        src_ref=gw.at[pl.ds(pl.multiple_of((1 - rep) * half, half), half), :],
        dst_ref=gw_in,
        send_sem=gw_send,
        recv_sem=gw_recv,
        device_id={"rep": 1 - rep},
        device_id_type=MESH,
    )
    swap.start()
    swap.wait()
    gw_out[...] = gw[pl.ds(pl.multiple_of(rep * half, half), half), :] + gw_in[...]

    for step in range(nz):
        ag_step(step, arrived=False, send=False)
    others = (n - 1) * rows
    for t, (ref, _) in enumerate(inputs):
        gone = ref.at[0, pl.ds(0, others), :]
        pltpu.make_async_copy(gone, gone, in_send.at[t]).wait()
    gone = m_buf.at[:, pl.ds(0, (n - 1) * cells)]
    pltpu.make_async_copy(gone, gone, m_send).wait()
    for t, (buf, out) in enumerate(outputs):
        gone = buf.at[:, pl.ds(0, (n - 1) * cells)]
        pltpu.make_async_copy(gone, gone, out_send.at[t]).wait()
        pltpu.make_async_copy(out, out, out_recv.at[t]).wait()


def on_device(n, queries, key_vectors, value_vectors, context, cotangent, out_weight, membership):
    ny = 2 if n == 8 else 1
    nz = n // ny
    features, cells = queries.shape[1], queries.shape[2]
    rows, length = features // n, cells * n
    heads = rows // DH
    low = jnp.bfloat16
    dma = pltpu.SemaphoreType.DMA
    anywhere = pl.BlockSpec(memory_space=pl.ANY)
    return pl.pallas_call(
        functools.partial(kernel, n, ny),
        out_shape=(
            jax.ShapeDtypeStruct(queries.shape, low),
            jax.ShapeDtypeStruct(queries.shape, low),
            jax.ShapeDtypeStruct(queries.shape, low),
            jax.ShapeDtypeStruct((rows // 2, features), jnp.float32),
        ),
        in_specs=[anywhere] * 7,
        out_specs=(anywhere, anywhere, anywhere, pl.BlockSpec(memory_space=pltpu.VMEM)),
        scratch_shapes=[pltpu.VMEM((rows, length), low)] * 8
        + [
            pltpu.VMEM((features, length), low),
            pltpu.VMEM((rows, features), low),
            pltpu.VMEM((1, length), jnp.int32),
            pltpu.VMEM((rows, features), jnp.float32),
            pltpu.VMEM((rows // 2, features), jnp.float32),
            pltpu.VMEM((DH, length), jnp.float32),
            pltpu.VMEM((DH, length), jnp.float32),
            dma, dma, dma, dma,
            dma((4,)), dma((4, heads)),
            dma((4, nz, CHUNKS)), dma((CHUNKS, n)),
            dma((3,)), dma((3,)),
            dma, dma,
        ],
        compiler_params=pltpu.CompilerParams(
            collective_id=0, has_side_effects=True, vmem_limit_bytes=56 << 20
        ),
    )(queries, key_vectors, value_vectors, context, cotangent, out_weight, membership)


def solution(mesh):
    cellwise = P(("grp", "rep"), None, "seq")
    return jax.shard_map(
        functools.partial(on_device, mesh.shape["seq"]),
        mesh=mesh,
        in_specs=(cellwise,) * 5 + (P("grp", None), P(("grp", "rep"), "seq")),
        out_specs=(cellwise, cellwise, cellwise, P(("grp", "seq", "rep"), None)),
        check_vma=False,
    )
```

```python
import functools
import math

import jax
import jax.numpy as jnp
from jax import lax
from jax.experimental import pallas as pl
from jax.experimental.pallas import tpu as pltpu
from jax.sharding import PartitionSpec as P

DH = 64
MESH = pl.DeviceIdType.MESH
CHUNKS = 4


def kernel(n, ny, *refs):
    (q_ref, k_ref, v_ref, c_ref, cot_ref, w_ref, m_ref,
     dq_out, dk_out, dv_out, gw_out,
     q_buf, k_buf, v_buf, c_buf, g_buf, dq_buf, dk_buf, dv_buf,
     cot, w_buf, m_buf, gw, gw_in, k_acc, v_acc,
     w_sem, own_sem, m_send, m_recv, in_send, in_recv,
     ag_send, ag_recv, out_send, out_recv, gw_send, gw_recv, gw_sem) = refs
    me = lax.axis_index("seq")
    rep = lax.axis_index("rep")
    nz = n // ny
    z, y = me // ny, me % ny
    rows, length = q_buf.shape
    cells = length // n
    features = cot.shape[0]
    heads = rows // DH
    half = rows // 2
    piece = features // CHUNKS
    inputs = ((k_ref, k_buf), (q_ref, q_buf), (v_ref, v_buf), (c_ref, c_buf))
    outputs = ((dv_buf, dv_out), (dq_buf, dq_out), (dk_buf, dk_out))

    def cols(seq):
        return pl.ds(pl.multiple_of(seq * cells, cells), cells)

    def head_rows(h, owner=0):
        return pl.ds(pl.multiple_of(owner * rows + h * DH, DH), DH)

    barrier = pltpu.get_barrier_semaphore()
    for k in range(1, n):
        pl.semaphore_signal(barrier, inc=1, device_id={"seq": (me + k) % n}, device_id_type=MESH)
    pl.semaphore_signal(barrier, inc=1, device_id={"rep": 1 - rep}, device_id_type=MESH)

    w_copy = pltpu.make_async_copy(
        w_ref.at[pl.ds(pl.multiple_of(me * rows, rows), rows), :], w_buf, w_sem
    )
    w_copy.start()
    own_copy = pltpu.make_async_copy(cot_ref.at[0], cot.at[:, cols(me)], own_sem)
    own_copy.start()
    pltpu.make_async_copy(m_ref, m_buf.at[:, cols(me)], m_recv).start()

    pl.semaphore_wait(barrier, n)

    def ag_copy(step, part, origin, way, target):
        part_rows = pl.ds(part * piece, piece)
        landing = cot.at[part_rows, cols(origin)]
        source = cot_ref.at[0, part_rows, :] if step == 0 else landing
        return pltpu.make_async_remote_copy(
            src_ref=source,
            dst_ref=landing,
            send_sem=ag_send.at[way, step, part],
            recv_sem=ag_recv.at[part, origin],
            device_id={"seq": target},
            device_id_type=MESH,
        )

    def ag_wait(part, origin):
        landing = cot.at[pl.ds(part * piece, piece), cols(origin)]
        pltpu.make_async_copy(landing, landing, ag_recv.at[part, origin]).wait()

    def ag_step(step, arrived, send):
        for part in range(CHUNKS):
            up, down = z - step, z + step

            def act(origin, way, target):
                copy = ag_copy(step, part, origin, way, target)
                if send:
                    copy.start()
                else:
                    copy.wait_send()

            def cross(origin, way):
                if ny == 2:
                    act(origin, way, z * ny + 1 - y)

            @pl.when(up >= 0)
            def _():
                if arrived:
                    ag_wait(part, up * ny + y)

                @pl.when(z + 1 < nz)
                def _():
                    act(up * ny + y, 0, me + ny)

                cross(up * ny + y, 2)

            @pl.when(down < nz)
            def _():
                if arrived:
                    ag_wait(part, down * ny + y)

                @pl.when(z >= 1)
                def _():
                    act(down * ny + y, 1, me - ny)

                if step > 0:
                    cross(down * ny + y, 3)

    def keep_inputs(h, carry):
        for t, (ref, buf) in enumerate(inputs):
            pltpu.make_async_copy(
                ref.at[0, head_rows(h, me), :], buf.at[head_rows(h), cols(me)], in_recv.at[t, h]
            ).start()
        return carry

    def send_inputs(h, column, first):
        def to_peer(k, carry):
            peer = (z + k) % nz * ny + column
            for t, (ref, buf) in enumerate(inputs):
                pltpu.make_async_remote_copy(
                    src_ref=ref.at[0, head_rows(h, peer), :],
                    dst_ref=buf.at[head_rows(h), cols(me)],
                    send_sem=in_send.at[t],
                    recv_sem=in_recv.at[t, h],
                    device_id={"seq": peer},
                    device_id_type=MESH,
                ).start()
            return carry

        lax.fori_loop(first, nz, to_peer, 0)

    def send_members(k, carry):
        pltpu.make_async_remote_copy(
            src_ref=m_ref,
            dst_ref=m_buf.at[:, cols(me)],
            send_sem=m_send,
            recv_sem=m_recv,
            device_id={"seq": (me + k) % n},
            device_id_type=MESH,
        ).start()
        return carry

    sent = 0
    for step in range(nz):
        ag_step(step, arrived=step > 0, send=True)
        if step == 0:
            lax.fori_loop(1, n, send_members, 0)
            lax.fori_loop(0, heads, keep_inputs, 0)
        upto = -(-(step + 1) * heads // nz)
        for h in range(sent, upto):
            send_inputs(h, y, 1)
            if ny == 2 and h > 0:
                send_inputs(h - 1, 1 - y, 0)
        sent = upto
    if ny == 2:
        send_inputs(heads - 1, 1 - y, 0)
    if ny == 2:
        for origin_z in range(nz):
            for part in range(CHUNKS):
                ag_wait(part, origin_z * ny + 1 - y)
    own_copy.wait()
    w_copy.wait()

    block = min(256, length)

    def project(i, carry):
        at = pl.ds(pl.multiple_of(i * block, block), block)
        g_buf[:, at] = jnp.dot(
            w_buf[...], cot[:, at], preferred_element_type=jnp.float32
        ).astype(jnp.bfloat16)
        return carry

    lax.fori_loop(0, length // block, project, 0)
    pltpu.make_async_copy(m_buf, m_buf, m_recv).wait()

    scale = 1.0 / math.sqrt(DH)
    tile = 256 if length <= 2048 else 128

    def one_head(h, carry):
        mine = head_rows(h)
        for t, (_, buf) in enumerate(inputs):
            pltpu.make_async_copy(buf.at[mine], buf.at[mine], in_recv.at[t, h]).wait()
        member = m_buf[...] > 0
        keys = k_buf[mine, :]
        values = v_buf[mine, :]
        keys_scaled = keys * jnp.bfloat16(scale)
        k_acc[...] = jnp.zeros_like(k_acc)
        v_acc[...] = jnp.zeros_like(v_acc)

        def one_tile(i, inner):
            at = pl.ds(pl.multiple_of(i * tile, tile), tile)
            query = q_buf[mine, at] * jnp.bfloat16(scale)
            grad = g_buf[mine, at]
            products = grad.astype(jnp.float32) * c_buf[mine, at].astype(jnp.float32)
            delta = jnp.sum(products.T, axis=1, keepdims=True)
            first = (((0,), (0,)), ((), ()))
            scores = lax.dot_general(query, keys, first, preferred_element_type=jnp.float32)
            scores = jnp.where(member, scores, -jnp.inf)
            exps = jnp.exp(scores - jnp.max(scores, axis=1, keepdims=True))
            probs = exps * (1.0 / jnp.sum(exps, axis=1, keepdims=True))
            v_acc[...] += jnp.dot(
                grad, probs.astype(jnp.bfloat16), preferred_element_type=jnp.float32
            )
            grad_probs = lax.dot_general(grad, values, first, preferred_element_type=jnp.float32)
            grad_scores = (probs * (grad_probs - delta)).astype(jnp.bfloat16)
            dq_buf[mine, at] = lax.dot_general(
                keys_scaled, grad_scores, (((1,), (1,)), ((), ())),
                preferred_element_type=jnp.float32,
            ).astype(jnp.bfloat16)
            k_acc[...] += jnp.dot(query, grad_scores, preferred_element_type=jnp.float32)
            return inner

        lax.fori_loop(0, length // tile, one_tile, 0)
        dk_buf[mine, :] = k_acc[...].astype(jnp.bfloat16)
        dv_buf[mine, :] = v_acc[...].astype(jnp.bfloat16)
        for t, (buf, out) in enumerate(outputs):
            pltpu.make_async_copy(
                buf.at[mine, cols(me)], out.at[0, head_rows(h, me), :], out_recv.at[t]
            ).start()

        def to_peer(k, inner):
            peer = (me + k) % n
            for t, (buf, out) in enumerate(outputs):
                pltpu.make_async_remote_copy(
                    src_ref=buf.at[mine, cols(peer)],
                    dst_ref=out.at[0, head_rows(h, me), :],
                    send_sem=out_send.at[t],
                    recv_sem=out_recv.at[t],
                    device_id={"seq": peer},
                    device_id_type=MESH,
                ).start()
            return inner

        lax.fori_loop(1, n, to_peer, 0)
        return carry

    lax.fori_loop(0, heads, one_head, 0)

    width = min(256, features)

    def weight_part(i, carry):
        at = pl.ds(pl.multiple_of(i * width, width), width)
        gw[:, at] = lax.dot_general(
            c_buf[...], cot[at, :], (((1,), (1,)), ((), ())), preferred_element_type=jnp.float32
        )
        return carry

    lax.fori_loop(0, features // width, weight_part, 0)
    swap = pltpu.make_async_remote_copy(
        src_ref=gw.at[pl.ds(pl.multiple_of((1 - rep) * half, half), half), :],
        dst_ref=gw_in,
        send_sem=gw_send,
        recv_sem=gw_recv,
        device_id={"rep": 1 - rep},
        device_id_type=MESH,
    )
    swap.start()
    swap.wait()
    gw_in[...] += gw[pl.ds(pl.multiple_of(rep * half, half), half), :]
    total = pltpu.make_async_copy(gw_in, gw_out, gw_sem)
    total.start()

    for step in range(nz):
        ag_step(step, arrived=False, send=False)
    others = (n - 1) * rows
    for t, (ref, _) in enumerate(inputs):
        gone = ref.at[0, pl.ds(0, others), :]
        pltpu.make_async_copy(gone, gone, in_send.at[t]).wait()
    gone = m_buf.at[:, pl.ds(0, (n - 1) * cells)]
    pltpu.make_async_copy(gone, gone, m_send).wait()
    for t, (buf, out) in enumerate(outputs):
        gone = buf.at[:, pl.ds(0, (n - 1) * cells)]
        pltpu.make_async_copy(gone, gone, out_send.at[t]).wait()
        pltpu.make_async_copy(out, out, out_recv.at[t]).wait()
    total.wait()


def hand_over(*refs):
    sources, targets, stages, (sem_in, sem_out) = refs[:4], refs[4:8], refs[8:12], refs[12:]
    reads, writes = [], []
    for t in range(4):
        reads.append(pltpu.make_async_copy(sources[t], stages[t], sem_in.at[t]))
        writes.append(pltpu.make_async_copy(stages[t], targets[t], sem_out.at[t]))
    for copy in reads:
        copy.start()
    for read, write in zip(reads, writes):
        read.wait()
        write.start()
    for copy in writes:
        copy.wait()


def on_device(n, queries, key_vectors, value_vectors, context, cotangent, out_weight, membership):
    ny = 2 if n == 8 else 1
    nz = n // ny
    features, cells = queries.shape[1], queries.shape[2]
    rows, length = features // n, cells * n
    heads = rows // DH
    low = jnp.bfloat16
    dma = pltpu.SemaphoreType.DMA
    anywhere = pl.BlockSpec(memory_space=pl.ANY)
    parts = pl.pallas_call(
        functools.partial(kernel, n, ny),
        out_shape=(
            jax.ShapeDtypeStruct(queries.shape, low),
            jax.ShapeDtypeStruct(queries.shape, low),
            jax.ShapeDtypeStruct(queries.shape, low),
            jax.ShapeDtypeStruct((rows // 2, features), jnp.float32),
        ),
        in_specs=[anywhere] * 7,
        out_specs=(anywhere,) * 4,
        scratch_shapes=[pltpu.VMEM((rows, length), low)] * 8
        + [
            pltpu.VMEM((features, length), low),
            pltpu.VMEM((rows, features), low),
            pltpu.VMEM((1, length), jnp.int32),
            pltpu.VMEM((rows, features), jnp.float32),
            pltpu.VMEM((rows // 2, features), jnp.float32),
            pltpu.VMEM((DH, length), jnp.float32),
            pltpu.VMEM((DH, length), jnp.float32),
            dma, dma, dma, dma,
            dma((4,)), dma((4, heads)),
            dma((4, nz, CHUNKS)), dma((CHUNKS, n)),
            dma((3,)), dma((3,)),
            dma, dma, dma,
        ],
        compiler_params=pltpu.CompilerParams(
            collective_id=0, has_side_effects=True, vmem_limit_bytes=56 << 20
        ),
    )(queries, key_vectors, value_vectors, context, cotangent, out_weight, membership)
    return pl.pallas_call(
        hand_over,
        out_shape=tuple(jax.ShapeDtypeStruct(part.shape, part.dtype) for part in parts),
        in_specs=[anywhere] * 4,
        out_specs=(anywhere,) * 4,
        scratch_shapes=[pltpu.VMEM(part.shape, part.dtype) for part in parts]
        + [dma((4,)), dma((4,))],
    )(*parts)


def solution(mesh):
    cellwise = P(("grp", "rep"), None, "seq")
    return jax.shard_map(
        functools.partial(on_device, mesh.shape["seq"]),
        mesh=mesh,
        in_specs=(cellwise,) * 5 + (P("grp", None), P(("grp", "rep"), "seq")),
        out_specs=(cellwise, cellwise, cellwise, P(("grp", "seq", "rep"), None)),
        check_vma=False,
    )
```

```python
import functools
import math

import jax
import jax.numpy as jnp
from jax import lax
from jax.experimental import pallas as pl
from jax.experimental.pallas import tpu as pltpu
from jax.sharding import PartitionSpec as P

DH = 64
MESH = pl.DeviceIdType.MESH
CHUNKS = 4


def kernel(n, ny, *refs):
    (q_ref, k_ref, v_ref, c_ref, cot_ref, w_ref, m_ref,
     dq_out, dk_out, dv_out, gw_out,
     q_buf, k_buf, v_buf, c_buf, g_buf, dq_buf, dk_buf, dv_buf,
     cot, w_buf, m_buf, gw, gw_in, k_acc, v_acc,
     w_sem, own_sem, m_send, m_recv, in_send, in_recv,
     ag_send, ag_recv, out_send, out_recv, gw_send, gw_recv, gw_sem) = refs
    me = lax.axis_index("seq")
    rep = lax.axis_index("rep")
    nz = n // ny
    z, y = me // ny, me % ny
    rows, length = q_buf.shape
    cells = length // n
    features = cot.shape[0]
    heads = rows // DH
    half = rows // 2
    piece = features // CHUNKS
    inputs = ((k_ref, k_buf), (q_ref, q_buf), (v_ref, v_buf), (c_ref, c_buf))
    outputs = ((dv_buf, dv_out), (dq_buf, dq_out), (dk_buf, dk_out))

    def cols(seq):
        return pl.ds(pl.multiple_of(seq * cells, cells), cells)

    def head_rows(h, owner=0):
        return pl.ds(pl.multiple_of(owner * rows + h * DH, DH), DH)

    barrier = pltpu.get_barrier_semaphore()
    for k in range(1, n):
        pl.semaphore_signal(barrier, inc=1, device_id={"seq": (me + k) % n}, device_id_type=MESH)
    pl.semaphore_signal(barrier, inc=1, device_id={"rep": 1 - rep}, device_id_type=MESH)

    w_copy = pltpu.make_async_copy(
        w_ref.at[pl.ds(pl.multiple_of(me * rows, rows), rows), :], w_buf, w_sem
    )
    w_copy.start()
    own_copy = pltpu.make_async_copy(cot_ref.at[0], cot.at[:, cols(me)], own_sem)
    own_copy.start()
    pltpu.make_async_copy(m_ref, m_buf.at[:, cols(me)], m_recv).start()

    pl.semaphore_wait(barrier, n)

    def ag_copy(step, part, origin, way, target):
        part_rows = pl.ds(part * piece, piece)
        landing = cot.at[part_rows, cols(origin)]
        source = cot_ref.at[0, part_rows, :] if step == 0 else landing
        return pltpu.make_async_remote_copy(
            src_ref=source,
            dst_ref=landing,
            send_sem=ag_send.at[way, step, part],
            recv_sem=ag_recv.at[part, origin],
            device_id={"seq": target},
            device_id_type=MESH,
        )

    def ag_wait(part, origin):
        landing = cot.at[pl.ds(part * piece, piece), cols(origin)]
        pltpu.make_async_copy(landing, landing, ag_recv.at[part, origin]).wait()

    def ag_step(step, arrived, send):
        for part in range(CHUNKS):
            up, down = z - step, z + step

            def act(origin, way, target):
                copy = ag_copy(step, part, origin, way, target)
                if send:
                    copy.start()
                else:
                    copy.wait_send()

            def cross(origin, way):
                if ny == 2:
                    act(origin, way, z * ny + 1 - y)

            @pl.when(up >= 0)
            def _():
                if arrived:
                    ag_wait(part, up * ny + y)

                @pl.when(z + 1 < nz)
                def _():
                    act(up * ny + y, 0, me + ny)

                cross(up * ny + y, 2)

            @pl.when(down < nz)
            def _():
                if arrived:
                    ag_wait(part, down * ny + y)

                @pl.when(z >= 1)
                def _():
                    act(down * ny + y, 1, me - ny)

                if step > 0:
                    cross(down * ny + y, 3)

    def keep_inputs(h, carry):
        for t, (ref, buf) in enumerate(inputs):
            pltpu.make_async_copy(
                ref.at[0, head_rows(h, me), :], buf.at[head_rows(h), cols(me)], in_recv.at[t, h]
            ).start()
        return carry

    def send_inputs(h, column, first):
        def to_peer(k, carry):
            peer = (z + k) % nz * ny + column
            for t, (ref, buf) in enumerate(inputs):
                pltpu.make_async_remote_copy(
                    src_ref=ref.at[0, head_rows(h, peer), :],
                    dst_ref=buf.at[head_rows(h), cols(me)],
                    send_sem=in_send.at[t],
                    recv_sem=in_recv.at[t, h],
                    device_id={"seq": peer},
                    device_id_type=MESH,
                ).start()
            return carry

        lax.fori_loop(first, nz, to_peer, 0)

    def send_members(k, carry):
        pltpu.make_async_remote_copy(
            src_ref=m_ref,
            dst_ref=m_buf.at[:, cols(me)],
            send_sem=m_send,
            recv_sem=m_recv,
            device_id={"seq": (me + k) % n},
            device_id_type=MESH,
        ).start()
        return carry

    sent = 0
    for step in range(nz):
        ag_step(step, arrived=step > 0, send=True)
        if step == 0:
            lax.fori_loop(1, n, send_members, 0)
            lax.fori_loop(0, heads, keep_inputs, 0)
        upto = -(-step * heads // nz)
        for h in range(sent, upto):
            for column, first in ((y, 1), (1 - y, 0))[:ny]:
                send_inputs(h, column, first)
        sent = upto
    for h in range(sent, heads):
        for column, first in ((y, 1), (1 - y, 0))[:ny]:
            send_inputs(h, column, first)
    if ny == 2:
        for origin_z in range(nz):
            for part in range(CHUNKS):
                ag_wait(part, origin_z * ny + 1 - y)
    own_copy.wait()
    w_copy.wait()

    block = min(256, length)

    def project(i, carry):
        at = pl.ds(pl.multiple_of(i * block, block), block)
        g_buf[:, at] = jnp.dot(
            w_buf[...], cot[:, at], preferred_element_type=jnp.float32
        ).astype(jnp.bfloat16)
        return carry

    lax.fori_loop(0, length // block, project, 0)
    pltpu.make_async_copy(m_buf, m_buf, m_recv).wait()

    scale = 1.0 / math.sqrt(DH)
    tile = 256 if length <= 2048 else 128

    def one_head(h, carry):
        mine = head_rows(h)
        for t, (_, buf) in enumerate(inputs):
            pltpu.make_async_copy(buf.at[mine], buf.at[mine], in_recv.at[t, h]).wait()
        member = m_buf[...] > 0
        keys = k_buf[mine, :]
        values = v_buf[mine, :]
        keys_scaled = keys * jnp.bfloat16(scale)
        k_acc[...] = jnp.zeros_like(k_acc)
        v_acc[...] = jnp.zeros_like(v_acc)

        def one_tile(i, inner):
            at = pl.ds(pl.multiple_of(i * tile, tile), tile)
            query = q_buf[mine, at] * jnp.bfloat16(scale)
            grad = g_buf[mine, at]
            products = grad.astype(jnp.float32) * c_buf[mine, at].astype(jnp.float32)
            delta = jnp.sum(products.T, axis=1, keepdims=True)
            first = (((0,), (0,)), ((), ()))
            scores = lax.dot_general(query, keys, first, preferred_element_type=jnp.float32)
            scores = jnp.where(member, scores, -jnp.inf)
            exps = jnp.exp(scores - jnp.max(scores, axis=1, keepdims=True))
            probs = exps * (1.0 / jnp.sum(exps, axis=1, keepdims=True))
            v_acc[...] += jnp.dot(
                grad, probs.astype(jnp.bfloat16), preferred_element_type=jnp.float32
            )
            grad_probs = lax.dot_general(grad, values, first, preferred_element_type=jnp.float32)
            grad_scores = (probs * (grad_probs - delta)).astype(jnp.bfloat16)
            dq_buf[mine, at] = lax.dot_general(
                keys_scaled, grad_scores, (((1,), (1,)), ((), ())),
                preferred_element_type=jnp.float32,
            ).astype(jnp.bfloat16)
            k_acc[...] += jnp.dot(query, grad_scores, preferred_element_type=jnp.float32)
            return inner

        lax.fori_loop(0, length // tile, one_tile, 0)
        dk_buf[mine, :] = k_acc[...].astype(jnp.bfloat16)
        dv_buf[mine, :] = v_acc[...].astype(jnp.bfloat16)
        for t, (buf, out) in enumerate(outputs):
            pltpu.make_async_copy(
                buf.at[mine, cols(me)], out.at[0, head_rows(h, me), :], out_recv.at[t]
            ).start()

        def to_peer(k, inner):
            peer = (me + k) % n
            for t, (buf, out) in enumerate(outputs):
                pltpu.make_async_remote_copy(
                    src_ref=buf.at[mine, cols(peer)],
                    dst_ref=out.at[0, head_rows(h, me), :],
                    send_sem=out_send.at[t],
                    recv_sem=out_recv.at[t],
                    device_id={"seq": peer},
                    device_id_type=MESH,
                ).start()
            return inner

        lax.fori_loop(1, n, to_peer, 0)
        return carry

    lax.fori_loop(0, heads, one_head, 0)

    width = min(256, features)

    def weight_part(i, carry):
        at = pl.ds(pl.multiple_of(i * width, width), width)
        gw[:, at] = lax.dot_general(
            c_buf[...], cot[at, :], (((1,), (1,)), ((), ())), preferred_element_type=jnp.float32
        )
        return carry

    lax.fori_loop(0, features // width, weight_part, 0)
    swap = pltpu.make_async_remote_copy(
        src_ref=gw.at[pl.ds(pl.multiple_of((1 - rep) * half, half), half), :],
        dst_ref=gw_in,
        send_sem=gw_send,
        recv_sem=gw_recv,
        device_id={"rep": 1 - rep},
        device_id_type=MESH,
    )
    swap.start()
    swap.wait()
    gw_in[...] += gw[pl.ds(pl.multiple_of(rep * half, half), half), :]
    total = pltpu.make_async_copy(gw_in, gw_out, gw_sem)
    total.start()

    for step in range(nz):
        ag_step(step, arrived=False, send=False)
    others = (n - 1) * rows
    for t, (ref, _) in enumerate(inputs):
        gone = ref.at[0, pl.ds(0, others), :]
        pltpu.make_async_copy(gone, gone, in_send.at[t]).wait()
    gone = m_buf.at[:, pl.ds(0, (n - 1) * cells)]
    pltpu.make_async_copy(gone, gone, m_send).wait()
    for t, (buf, out) in enumerate(outputs):
        gone = buf.at[:, pl.ds(0, (n - 1) * cells)]
        pltpu.make_async_copy(gone, gone, out_send.at[t]).wait()
        pltpu.make_async_copy(out, out, out_recv.at[t]).wait()
    total.wait()


def hand_over(*refs):
    sources, targets, stages, (sem_in, sem_out) = refs[:4], refs[4:8], refs[8:12], refs[12:]
    reads, writes = [], []
    for t in range(4):
        reads.append(pltpu.make_async_copy(sources[t], stages[t], sem_in.at[t]))
        writes.append(pltpu.make_async_copy(stages[t], targets[t], sem_out.at[t]))
    for copy in reads:
        copy.start()
    for read, write in zip(reads, writes):
        read.wait()
        write.start()
    for copy in writes:
        copy.wait()


def on_device(n, queries, key_vectors, value_vectors, context, cotangent, out_weight, membership):
    ny = 2 if n == 8 else 1
    nz = n // ny
    features, cells = queries.shape[1], queries.shape[2]
    rows, length = features // n, cells * n
    heads = rows // DH
    low = jnp.bfloat16
    dma = pltpu.SemaphoreType.DMA
    anywhere = pl.BlockSpec(memory_space=pl.ANY)
    parts = pl.pallas_call(
        functools.partial(kernel, n, ny),
        out_shape=(
            jax.ShapeDtypeStruct(queries.shape, low),
            jax.ShapeDtypeStruct(queries.shape, low),
            jax.ShapeDtypeStruct(queries.shape, low),
            jax.ShapeDtypeStruct((rows // 2, features), jnp.float32),
        ),
        in_specs=[anywhere] * 7,
        out_specs=(anywhere,) * 4,
        scratch_shapes=[pltpu.VMEM((rows, length), low)] * 8
        + [
            pltpu.VMEM((features, length), low),
            pltpu.VMEM((rows, features), low),
            pltpu.VMEM((1, length), jnp.int32),
            pltpu.VMEM((rows, features), jnp.float32),
            pltpu.VMEM((rows // 2, features), jnp.float32),
            pltpu.VMEM((DH, length), jnp.float32),
            pltpu.VMEM((DH, length), jnp.float32),
            dma, dma, dma, dma,
            dma((4,)), dma((4, heads)),
            dma((4, nz, CHUNKS)), dma((CHUNKS, n)),
            dma((3,)), dma((3,)),
            dma, dma, dma,
        ],
        compiler_params=pltpu.CompilerParams(
            collective_id=0, has_side_effects=True, vmem_limit_bytes=56 << 20
        ),
    )(queries, key_vectors, value_vectors, context, cotangent, out_weight, membership)
    return pl.pallas_call(
        hand_over,
        out_shape=tuple(jax.ShapeDtypeStruct(part.shape, part.dtype) for part in parts),
        in_specs=[anywhere] * 4,
        out_specs=(anywhere,) * 4,
        scratch_shapes=[pltpu.VMEM(part.shape, part.dtype) for part in parts]
        + [dma((4,)), dma((4,))],
    )(*parts)


def solution(mesh):
    cellwise = P(("grp", "rep"), None, "seq")
    return jax.shard_map(
        functools.partial(on_device, mesh.shape["seq"]),
        mesh=mesh,
        in_specs=(cellwise,) * 5 + (P("grp", None), P(("grp", "rep"), "seq")),
        out_specs=(cellwise, cellwise, cellwise, P(("grp", "seq", "rep"), None)),
        check_vma=False,
    )
```
